256 devices in a mesh: tm: 4 (over y), lag: 64 (over x, z, core).
Axes of the slice: x: 4, y: 4, z: 8, core: 2. Of those that a mesh axis runs over, the one named last changes fastest.
Arguments:
- samples: bfloat16 [8192, 512], P(('tm', 'lag')), may hold values from -6 to 6
Outputs:
- upper_gen: float32 [128, 512, 512], P('lag', None, 'tm')
- lower_gen: float32 [128, 512, 512], P('lag', None, 'tm')
The draws below stay inside these ranges and needn't reach their ends.
All inputs are finite; a program needn't handle non-finite values.
Results may differ from the reference program's by a relative error of at most 0.0003.
Values may be sent and summed in bfloat16 or wider, within the bound.
No kernel may reach another device: no remote copies, remote signals or barrier semaphores. Data moves between devices by JAX's collectives and lax.ppermute only.
A program may use at most 64 MiB of HBM per device.

```python
import jax
import jax.numpy as jnp
from jax import lax

C = 512
LAG_DEV = 2
TIME = 8192
SCHUR_STEPS = 3
N_LAG = 64


def block_scale(key, dims, split, low, largest):
    gain = 1.0
    for position, shards_of in split:
        heights = jax.random.uniform(jax.random.fold_in(jax.random.fold_in(key, 6), position), (shards_of,), jnp.float32, low / len(split), largest / len(split))
        gain = gain * jnp.repeat(jnp.exp(heights), dims[position] // shards_of).reshape((-1,) + (1,) * (len(dims) - 1 - position))
    return gain


def bell_draw(rng, dims, scale, reach, pieces=(), held_as=jnp.bfloat16):
    array = jax.random.normal(rng, dims, jnp.float32) * scale
    if len(pieces) > 0:
        array = block_scale(rng, dims, pieces, -0.22, 0.18) * array
    return jnp.clip(array, min=-reach, max=reach).astype(held_as)


def setup_inputs(seed: int = 0) -> dict:
    splits = jax.random.split(jax.random.key(seed), 2)
    samples = bell_draw(splits[0], (TIME, C), 1.0, 6.0, ((0, 256),))
    return {"samples": samples}


HIGH = lax.Precision.HIGHEST

def lag_products(samples):
    total_lags = LAG_DEV * N_LAG
    values = samples.astype(jnp.float32)
    padded = jnp.concatenate([values, jnp.zeros((total_lags, C), jnp.float32)], axis=0)

    def one_lag(lag_index):
        shifted = lax.dynamic_slice_in_dim(padded, lag_index, TIME, 0)
        return lax.dot_general(shifted.astype(jnp.float32), values.astype(jnp.float32), (((0,), (0,)), ((), ())), precision=HIGH, preferred_element_type=jnp.float32)
    return lax.map(one_lag, jnp.arange(total_lags, dtype=jnp.int32)) / jnp.float32(TIME)

def reflection(head, lower_head):
    return jnp.linalg.solve(head.T, lower_head.T).T

def reference(samples):
    blocks = lag_products(samples)
    total_lags = blocks.shape[0]
    first = (jnp.arange(total_lags) == 0)[:, None, None]
    upper = blocks
    lower = jnp.where(first, jnp.zeros_like(blocks), blocks)
    for schur_step in range(1, SCHUR_STEPS + 1):
        upper = jnp.concatenate([jnp.zeros_like(upper[:1]), upper[:-1]], axis=0)
        coeff = reflection(upper[schur_step], lower[schur_step])
        new_upper = upper - jnp.einsum('ab,kac->kbc', coeff, lower, precision=HIGH)
        lower = lower - jnp.einsum('ab,kbc->kac', coeff, upper, precision=HIGH)
        upper = new_upper
    return (upper, lower)
```

```python
import functools

import jax
import jax.numpy as jnp
from jax import lax
from jax.experimental import pallas as pl
from jax.experimental.pallas import tpu as pltpu
from jax.sharding import Mesh, PartitionSpec as P

C = 512
LAG_DEV = 2
TIME = 8192
SCHUR_STEPS = 3
BLOCK = 512
HALF = 256
PIECES = (
    (0, (0, -1, 1, 2)),
    (-1, (0, -1, 1, 2)),
    (1, (0, -1, 1, 2)),
    (2, (0, -1)),
    (2, (1, 2)),
)
CHUNK = 2048
PAD = 128
SHARE = 128
LOCAL = LAG_DEV + SCHUR_STEPS
ACCEPT = 1e-4

F32, BF16 = jnp.float32, jnp.bfloat16
HIGHEST = lax.Precision.HIGHEST


def mm(a, b):
    return jnp.dot(a, b, preferred_element_type=F32)


def mm_nt(a, b):
    return lax.dot_general(a, b, (((1,), (1,)), ((), ())), preferred_element_type=F32)


def halves(value):
    high = value.astype(BF16)
    return high, (value - high.astype(F32)).astype(BF16)


def mm3(a, b):
    return mm(a[0], b[0]) + mm(a[0], b[1]) + mm(a[1], b[0])


def eye():
    rows = lax.broadcasted_iota(jnp.int32, (C, C), 0)
    cols = lax.broadcasted_iota(jnp.int32, (C, C), 1)
    return jnp.where(rows == cols, 1.0, 0.0).astype(F32)


def load_blocks(place, sources, xt, sem):
    y, x, core = place[0], place[2], place[3]
    copies = []
    for whose in range(2):
        colour = lax.rem(core + whose, 2)
        for source, (far, nears) in zip(sources[whose], PIECES, strict=True):
            for i, near in enumerate(nears):
                along_x = lax.rem(x + jnp.where(colour == 0, near, far) + 4, 4)
                along_y = lax.rem(y + jnp.where(colour == 0, far, near) + 4, 4)
                start = PAD + (along_y * 4 + along_x) * BLOCK + colour * HALF
                to = xt.at[:, pl.ds(pl.multiple_of(start, HALF // 2), HALF)]
                copies.append(
                    pltpu.make_async_copy(source.at[i], to, sem.at[len(copies)])
                )
    return copies


def products(place, xt, moved, columns, heads, local):
    lag0 = LAG_DEV * place[1] - SCHUR_STEPS
    first = pl.multiple_of(place[0] * SHARE, SHARE)
    wide = CHUNK + PAD
    heads[...] = jnp.zeros_like(heads)
    local[...] = jnp.zeros_like(local)

    def chunk_step(c, carry):
        start = pl.multiple_of(c * CHUNK, CHUNK)
        for shift in range(1, SCHUR_STEPS + 1):
            for row in range(0, C, 128):
                ext = xt[row : row + 128, pl.ds(start + PAD, wide)].astype(F32)
                rolled = pltpu.roll(ext, wide - shift, 1)
                moved[shift - 1, row : row + 128, :] = rolled[:, :CHUNK].astype(BF16)
        for j in range(LOCAL):
            ext = xt[pl.ds(first, SHARE), pl.ds(start, wide)].astype(F32)
            rolled = pltpu.roll(ext, CHUNK + lag0 + j, 1)
            columns[j * SHARE : (j + 1) * SHARE, :] = rolled[:, :CHUNK].astype(BF16)
        still = xt[:, pl.ds(start + PAD, CHUNK)]
        heads[0] += mm_nt(still, still)
        for shift in range(1, SCHUR_STEPS + 1):
            heads[shift] += mm_nt(moved[shift - 1], still)
        local[...] += mm_nt(still, columns[...])
        return carry

    lax.fori_loop(0, TIME // CHUNK, chunk_step, 0)
    scale = 1.0 / TIME
    heads[...] = heads[...] * scale
    for j in range(LOCAL):
        keep = jnp.where(lag0 + j >= 0, scale, 0.0)
        part = slice(j * SHARE, (j + 1) * SHARE)
        local[:, part] = local[:, part] * keep


def rows_product(out, left, right, finish):
    def step(i, carry):
        rows = pl.ds(pl.multiple_of(i * 128, 128), 128)
        value = jnp.dot(
            left[rows, :], right[...], precision=HIGHEST, preferred_element_type=F32
        )
        out[rows, :] = finish(value, rows)
        return carry

    lax.fori_loop(0, C // 128, step, 0)


def careful_solve(upper, lower, coeff, inverse, work, spare):
    head = upper[...]
    size = jnp.abs(head)
    bound = jnp.max(jnp.sum(size, axis=0)) * jnp.max(jnp.sum(size, axis=1))
    inverse[...] = head.T / bound

    def error(value, rows):
        place = rows.start + lax.broadcasted_iota(jnp.int32, (128, C), 0)
        cols = lax.broadcasted_iota(jnp.int32, (128, C), 1)
        return jnp.where(place == cols, 1.0, 0.0) - value

    def more(state):
        count, norm = state
        return jnp.logical_and(count < 100, norm > 1e-5)

    def newton(state):
        count, _ = state
        rows_product(work, upper, inverse, error)
        rows_product(spare, inverse, work, lambda v, rows: v + inverse[rows, :])
        inverse[...] = spare[...]
        return count + 1, jnp.sum(work[...] * work[...])

    lax.while_loop(more, newton, (0, jnp.float32(1e30)))
    rows_product(coeff, lower, inverse, lambda v, rows: v)
    rows_product(work, coeff, upper, lambda v, rows: lower[rows, :] - v)
    rows_product(spare, work, inverse, lambda v, rows: v + coeff[rows, :])
    coeff[...] = spare[...]


def solve(upper, lower, near, coeff, inverse, work, spare):
    low = lower[...]
    guess = mm(low.astype(BF16), near).astype(BF16)
    high, rest = halves(upper[...])
    left = low - mm(guess, high) - mm(guess, rest)
    error, size = jnp.sum(left * left), jnp.sum(low * low)
    coeff[...] = guess.astype(F32) + mm(left.astype(BF16), near)

    @pl.when(jnp.logical_not(error <= ACCEPT * size))
    def _():
        careful_solve(upper, lower, coeff, inverse, work, spare)


def kernel(place, *refs):
    sources = (refs[:5], refs[5:10])
    (out_upper, out_lower, xt, moved, columns, heads, local,
     up, low, near, coeff, inverse, work, spare, sem) = refs[10:]
    copies = load_blocks(place, sources, xt, sem)
    for copy in copies:
        copy.start()
    xt[:, :PAD] = jnp.zeros((C, PAD), BF16)
    xt[:, PAD + TIME :] = jnp.zeros((C, PAD), BF16)
    for copy in copies:
        copy.wait()
    products(place, xt, moved, columns, heads, local)

    one = eye()
    head = heads[0]
    weight = jnp.sum(head * one) / jnp.sum(head * head)
    err = (one - weight * head)
    err_b = err.astype(BF16)
    inv = weight * (one + err)
    err2 = mm(err_b, err_b).astype(BF16)
    inv = inv + mm(inv.astype(BF16), err2)
    err4 = mm(err2, err2).astype(BF16)
    inv = inv + mm(inv.astype(BF16), err4)
    near[...] = inv.astype(BF16)
    solve(heads.at[0], heads.at[1], near[...], coeff, inverse, work, spare)

    lag0 = LAG_DEV * place[1] - SCHUR_STEPS
    k = coeff[...]
    straight, turned = halves(k), halves(k.T)
    r1, r2 = halves(heads[1]), halves(heads[2])
    up[0] = heads[0] - mm3(turned, r1)
    up[1] = heads[1] - mm3(turned, r2)
    low[0] = heads[2] - mm3(straight, r1)
    low[1] = heads[3] - mm3(straight, r2)
    uppers = local[...]
    column = lax.broadcasted_iota(jnp.int32, (C, LOCAL * SHARE), 1)
    zero_lag = column // SHARE == -lag0
    lowers = jnp.where(zero_lag, 0.0, uppers)
    u = uppers[:, : 3 * SHARE] - mm3(turned, halves(lowers[:, SHARE : 4 * SHARE]))
    l = lowers[:, 2 * SHARE :] - mm3(straight, halves(uppers[:, SHARE : 4 * SHARE]))

    def closer(upper):
        before = near[...]
        err = one - mm(upper.astype(BF16), before)
        err_b = err.astype(BF16)
        inv = before.astype(F32) + mm(before, err_b)
        err2 = mm(err_b, err_b).astype(BF16)
        inv = inv + mm(inv.astype(BF16), err2)
        near[...] = inv.astype(BF16)

    closer(up[0])
    solve(up.at[0], low.at[0], near[...], coeff, inverse, work, spare)
    k = coeff[...]
    straight, turned = halves(k), halves(k.T)
    low[1] = low[1] - mm3(straight, halves(up[1]))
    up[0] = up[0] - mm3(turned, halves(low[0]))
    u, l = (
        u[:, : 2 * SHARE] - mm3(turned, halves(l[:, : 2 * SHARE])),
        l[:, SHARE:] - mm3(straight, halves(u[:, SHARE:])),
    )

    closer(up[0])
    solve(up.at[0], low.at[1], near[...], coeff, inverse, work, spare)
    k = coeff[...]
    straight, turned = halves(k), halves(k.T)
    u, l = u - mm3(turned, halves(l)), l - mm3(straight, halves(u))
    for i in range(LAG_DEV):
        out_upper[i] = u[:, i * SHARE : (i + 1) * SHARE]
        out_lower[i] = l[:, i * SHARE : (i + 1) * SHARE]


def eliminate(place, pieces):
    square = pltpu.VMEM((C, C), F32)
    out = jax.ShapeDtypeStruct((LAG_DEV, C, SHARE), F32)
    return pl.pallas_call(
        kernel,
        out_shape=(out, out),
        in_specs=[
            pl.BlockSpec(memory_space=pltpu.SMEM),
            *([pl.BlockSpec(memory_space=pl.ANY)] * len(pieces)),
        ],
        out_specs=(pl.BlockSpec(memory_space=pltpu.VMEM),) * 2,
        scratch_shapes=[
            pltpu.VMEM((C, PAD + TIME + PAD), BF16),
            pltpu.VMEM((SCHUR_STEPS, C, CHUNK), BF16),
            pltpu.VMEM((LOCAL * SHARE, CHUNK), BF16),
            pltpu.VMEM((4, C, C), F32),
            pltpu.VMEM((C, LOCAL * SHARE), F32),
            pltpu.VMEM((2, C, C), F32),
            pltpu.VMEM((2, C, C), F32),
            pltpu.VMEM((C, C), BF16),
            square,
            square,
            square,
            square,
            pltpu.SemaphoreType.DMA((TIME // HALF,)),
        ],
        compiler_params=pltpu.CompilerParams(vmem_limit_bytes=60 << 20),
        name="eliminate",
    )(place, *pieces)


AXES = ("y", "x", "z", "c")


def routes(sizes, move):
    y, x, z, c = sizes
    number = lambda p: ((p[0] % y * x + p[1] % x) * z + p[2] % z) * c + p[3] % c
    places = [
        (i, j, k, l) for i in range(y) for j in range(x) for k in range(z) for l in range(c)
    ]
    return [(number(p), number(move(*p))) for p in places]


def shards(sizes, samples):
    def along(axis, step):
        return routes(
            sizes,
            lambda y, x, z, c: (y, x + step, z, c) if c == axis else (y + step, x, z, c),
        )

    other = routes(sizes, lambda y, x, z, c: (y, x, z, 1 - c))
    send = lambda value, route: lax.ppermute(value, AXES, route)
    core = lax.axis_index("c")
    many = sizes[2] * sizes[3]
    block = lax.all_to_all(
        jnp.broadcast_to(samples[None], (many, *samples.shape)), ("z", "c"), 0, 0
    )
    block = block.reshape(BLOCK, C).T
    own = lax.dynamic_slice_in_dim(block, core * HALF, HALF, 1)

    before, after = send(own, along(0, 1)), send(own, along(0, -1))
    top, bottom = send(before[:HALF], along(0, 1)), send(after[HALF:], along(0, -1))
    across = jnp.concatenate([top, bottom], axis=0)
    own = jnp.stack([own, before, after, across])

    before, after = send(own, along(1, 1)), send(own, along(1, -1))
    own_other = send(own, other)
    top, bottom = send(before[:2], along(1, 1)), send(after[2:], along(1, -1))
    before_other, after_other = send(before, other), send(after, other)
    mine = (own, before, after, top, bottom)
    others = (own_other, before_other, after_other, send(top, other), send(bottom, other))
    place = jnp.stack(
        [
            lax.axis_index("y"),
            lax.axis_index(("x", "z", "c")),
            lax.axis_index("x"),
            core,
        ]
    ).astype(jnp.int32)
    return eliminate(place, mine + others)


def solution(mesh):
    sizes = (4, 4, 8, 2)
    fine = Mesh(mesh.devices.reshape(sizes), AXES)
    return jax.shard_map(
        functools.partial(shards, sizes),
        mesh=fine,
        in_specs=(P(AXES, None),),
        out_specs=(P(("x", "z", "c"), None, "y"),) * 2,
        check_vma=False,
    )
```
